32 devices in a mesh: band: 8 (over y, x, core), pair: 4 (over z).
Axes of the slice: x: 2, y: 2, z: 4, core: 2. Of those that a mesh axis runs over, the one named last changes fastest.
Arguments:
- orbitals: bfloat16 [16, 32, 1024], P('band'), may hold values from -6 to 6
- kernel: float32 [32, 1024], replicated, may hold values from 0 to 1.2, as said below
- occupations: float32 [16], replicated, may hold values from 0.04 to 0.99
- plan: int32 [8], replicated, may hold values from 0 to 7, each once
Outputs:
- exchange: float32 [16, 32, 1024], P('band', 'pair')
- slot_energy: float32 [8], P('pair')
The draws below stay inside these ranges and needn't reach their ends.
Inputs may be any that keep to these rules, and one draw needn't show every extreme that they name: `plan`: each owner distance 0 to 7 appears exactly once. kernel is unchanged when any one frequency index i is replaced by (32 - i) % 32, and is not negative.
All inputs are finite; a program needn't handle non-finite values.
Results may differ from the reference program's by a relative error of at most 0.0004.
Values may be sent and summed in bfloat16 or wider, within the bound.
A program may use at most 64 MiB of HBM per device.

```python
import math
import jax
import jax.numpy as jnp
from jax import lax

L = 32
ORB_DEV = 2
ORBITALS = 16
N_BAND = 8


def draw_kernel(key, part):
    half = L // 2
    key_radius, key_rough = jax.random.split(jax.random.fold_in(key, 11))
    radius = jax.random.uniform(key_radius, (), jnp.float32, 1.5, 3.0)
    rough = jax.random.uniform(key_rough, (half + 1, half + 1, half + 1), jnp.float32, 0.8, 1.2)
    index = jnp.arange(L, dtype=jnp.int32)
    folded = jnp.where(index <= half, index, L - index)
    wave = folded.astype(jnp.float32) * (2.0 * math.pi / L)
    squared = wave[:, None, None] ** 2 + wave[None, :, None] ** 2 + wave[None, None, :] ** 2
    scaled = jnp.sqrt(squared) * radius
    safe = jnp.maximum(scaled, 0.001)
    base = jnp.where(scaled < 0.001, 1.0, 2.0 * (1.0 - jnp.cos(safe)) / (safe * safe))
    factor = rough[folded][:, folded][:, :, folded]
    return (base * factor).reshape(L, L * L)


def draw_occupations(key, part):
    noise = jax.random.uniform(jax.random.fold_in(key, 23), (ORBITALS,), jnp.float32, -0.3, 0.3)
    level = jnp.linspace(-2.5, 1.5, ORBITALS) + noise
    return jax.nn.sigmoid(-level)


def shard_levels(stream_key, extent, cuts, smallest, high):
    factor_of = 1.0
    for axis_at, blocks in cuts:
        steps = jax.random.uniform(jax.random.fold_in(jax.random.fold_in(stream_key, 6), axis_at), (blocks,), jnp.float32, smallest / len(cuts), high / len(cuts))
        factor_of = factor_of * jnp.repeat(jnp.exp(steps), extent[axis_at] // blocks).reshape((-1,) + (1,) * (len(extent) - 1 - axis_at))
    return factor_of


def bell_draw(own_key, extent, spread, reach, shards=(), kind=jnp.bfloat16):
    result = spread * jax.random.normal(own_key, extent, jnp.float32)
    if shards:
        result = result * shard_levels(own_key, extent, shards, -0.22, 0.18)
    return jnp.clip(result, -reach, reach).astype(kind)


def setup_inputs(seed: int = 0) -> dict:
    seeds = jax.random.split(jax.random.key(seed), 5)
    orbitals = bell_draw(seeds[0], (ORBITALS, L, L * L), 1.0, 6.0, ((0, 8),))
    kernel = draw_kernel(jax.random.fold_in(seeds[4], 71), 0)
    occupations = draw_occupations(jax.random.fold_in(seeds[4], 71), 0)
    plan = jax.random.permutation(seeds[3], N_BAND).astype(jnp.int32)
    return dict(orbitals=orbitals, kernel=kernel, occupations=occupations, plan=plan)


def reference(orbitals, kernel, occupations, plan):
    fields = orbitals.astype(jnp.float32).reshape(ORBITALS, L, L, L)
    multiplier = kernel.reshape(L, L, L)[:, :, : L // 2 + 1]
    weighted = fields * occupations[:, None, None, None]

    def one_orbital(target):
        density = fields * target[None]
        spectrum = jnp.fft.rfftn(density, axes=(1, 2, 3))
        potential = jnp.fft.irfftn(spectrum * multiplier[None], s=(L, L, L), axes=(1, 2, 3))
        applied = -jnp.sum(potential * weighted, axis=0)
        inner = jnp.sum(potential * density, axis=(1, 2, 3))
        return applied, inner

    applied, inner = lax.map(one_orbital, fields)
    pair_sum = occupations[:, None] * occupations[None, :] * inner
    owner = jnp.arange(ORBITALS, dtype=jnp.int32) // ORB_DEV
    distance = jnp.bitwise_xor(owner[:, None], owner[None, :])
    levels = jnp.arange(N_BAND, dtype=jnp.int32)
    onehot = (distance[:, :, None] == levels[None, None, :]).astype(jnp.float32)
    by_distance = jnp.sum(pair_sum[:, :, None] * onehot, axis=(0, 1))
    pick = (plan[:, None] == levels[None, :]).astype(jnp.float32)
    slot_energy = -jnp.sum(pick * by_distance[None, :], axis=1) / (2.0 * ORBITALS * L ** 3)
    return applied.reshape(ORBITALS, L, L * L), slot_energy
```

```python
import functools
import math

import jax
import jax.numpy as jnp
import ml_dtypes
import numpy as np
from jax import lax
from jax.experimental import pallas as pl
from jax.experimental.pallas import tpu as pltpu
from jax.sharding import PartitionSpec as P

MESH = pl.DeviceIdType.MESH
F32 = jnp.float32
BF16 = jnp.bfloat16


def pieces(value, count):
    terms = []
    for at in range(count):
        term = value.astype(BF16)
        terms.append(term)
        if at < count - 1:
            value = value - term.astype(F32)
    return terms


def tables(points):
    half = points // 2
    block = half * half
    sw, row, col = (x.reshape(-1) for x in np.meshgrid(np.arange(2), np.arange(half), np.arange(half), indexing="ij"))
    target = np.arange(2 * block)
    place = np.where(sw == 0, col, points - 1 - col)
    fold = np.zeros((2, 2 * block, 2 * block), np.float32)
    fold[0, row * points + place, target] = 1.0
    fold[1, (half - 1 - row) * points + place, target] = 1.0
    select = np.zeros((2 * block, 2 * block), np.float32)
    select[row * points + col + sw, target] = 1.0
    spot = np.arange(half) + 0.5
    basis = []
    for odd in range(2):
        mode = np.arange(half) + odd
        angle = 2.0 * np.pi * mode[:, None] * spot[None, :] / points
        edge = (mode == 0) | (mode == half)
        factor = np.where(edge, math.sqrt(1.0 / half), math.sqrt(2.0 / half))
        basis.append((np.sin(angle) if odd else np.cos(angle)) * factor[:, None])
    joint = np.stack([np.kron(basis[v], basis[w]).T for v in range(2) for w in range(2)])
    high = joint.astype(ml_dtypes.bfloat16)
    low = (joint - high.astype(np.float64)).astype(ml_dtypes.bfloat16)
    shift = np.arange(-(-(half + 1) // 8) * 8)
    cosine = np.cos(2.0 * np.pi * shift[:, None] * np.arange(points)[None, :] / points) / (4.0 * points)
    maps = np.concatenate([fold, select[None]]).astype(ml_dtypes.bfloat16)
    return maps, np.stack([high, low]), cosine.astype(np.float32)


def kernel(
    dims,
    plan_ref, occ_ref, orb_ref, ker_ref, cos_ref, maps_hbm, joint_hbm,
    out_ref, slot_ref,
    held, maps, joint, left, right, spread, lhs, spectrum, field, total, tile, sums, band_in, pair_in,
    load_sem, send_sem, recv_sem, band_send, band_recv, pair_send, pair_recv,
):
    n_band, n_pair, points, per_owner = dims
    meets = n_band // n_pair
    plane = points * points
    half = points // 2
    block = half * half
    planes = points // n_pair
    pairs = per_owner * per_owner * meets
    rows = points * pairs
    me = lax.axis_index("band")
    group = lax.axis_index("pair")
    base = group * planes

    loads = [
        pltpu.make_async_copy(maps_hbm, maps, load_sem.at[0]),
        pltpu.make_async_copy(joint_hbm, joint, load_sem.at[1]),
    ]
    for load in loads:
        load.start()

    barrier = pltpu.get_barrier_semaphore()
    for x in range(1, n_band):
        pl.semaphore_signal(barrier, inc=1, device_id={"band": me ^ x}, device_id_type=MESH)
    for x in range(1, n_pair):
        pl.semaphore_signal(barrier, inc=1, device_id={"pair": group ^ x}, device_id_type=MESH)
    pl.semaphore_wait(barrier, n_band + n_pair - 2)

    def order(step):
        first = jnp.maximum(group, 1) - 1
        return jnp.where(step == 0, 0, 1 + lax.rem(first + step - 1 + (n_pair - 1), n_pair - 1))

    def move(src, chunk, member, target):
        return pltpu.make_async_remote_copy(
            src_ref=src,
            dst_ref=held.at[chunk, member],
            send_sem=send_sem.at[chunk, member],
            recv_sem=recv_sem.at[chunk, member],
            device_id={"band": target},
            device_id_type=MESH,
        )

    for m in range(1, meets):
        move(orb_ref, 0, m, me ^ m).start()

    def send_direct(step, carry):
        chunk = order(step)
        move(orb_ref, chunk, 0, me ^ (chunk * meets)).start()
        return carry

    lax.fori_loop(1, n_pair, send_direct, 0)

    held[0, 0] = orb_ref[...]
    total[...] = jnp.zeros_like(total)

    mixed = jnp.dot(cos_ref[...], ker_ref[...], precision=lax.Precision.HIGHEST, preferred_element_type=F32)
    shifted = pltpu.roll(mixed, plane - points, 1)
    loads[0].wait()
    for v, source in enumerate((mixed, shifted)):
        picked = 0.0
        for term in pieces(source[:, : 2 * block], 3):
            picked = picked + jnp.dot(term, maps[2], preferred_element_type=F32)
        for s in range(half + 1):
            spread[s, :, v * 2 * block : (v + 1) * 2 * block] = jnp.broadcast_to(
                picked[s : s + 1], (8, 2 * block)
            )

    def folded(raw):
        return [
            jnp.dot(raw[:, v * 2 * block : (v + 1) * 2 * block], maps[v], preferred_element_type=F32)
            for v in range(2)
        ]

    own = folded(orb_ref[...].reshape(per_owner * points, plane))
    per_a = meets * per_owner
    for a in range(per_owner):
        for v in range(2):
            value = own[v][a * points : (a + 1) * points]
            for o in range(per_a):
                left[:, a * per_a + o, v * 2 * block : (v + 1) * 2 * block] = value
    loads[1].wait()

    sub = lax.broadcasted_iota(jnp.int32, (pairs, 128), 0)

    def convolve(start, t):
        lanes = slice(t * 128, (t + 1) * 128)
        y = [spectrum[lax.rem(start + i, points), :, lanes] for i in range(points)]
        z = []
        for j in range(planes):
            value = spread[0, :, lanes] * y[j] + spread[half, :, lanes] * y[(j + half) % points]
            for s in range(1, half):
                value = value + spread[s, :, lanes] * (y[(j + s) % points] + y[(j - s) % points])
            z.append(value)
        return y, z

    def step_body(step, carry):
        chunk = order(step)

        @pl.when(step == 2)
        def _():
            for x in range(1, n_band):
                pltpu.make_async_remote_copy(
                    src_ref=tile, dst_ref=band_in.at[x], send_sem=band_send.at[x], recv_sem=band_recv.at[x],
                    device_id={"band": me ^ x}, device_id_type=MESH,
                ).start()

        for m in range(1, meets):
            move(orb_ref, chunk, m, me ^ m).wait_recv()
        moved = folded(held[chunk].reshape(meets * per_owner * points, plane))
        for v in range(2):
            for o in range(per_a):
                value = moved[v][o * points : (o + 1) * points]
                for a in range(per_owner):
                    right[:, a * per_a + o, v * 2 * block : (v + 1) * 2 * block] = value

        density = (left[...] * right[...]).reshape(rows, plane)
        part = [density[:, q * block : (q + 1) * block] for q in range(4)]
        s0, d0 = part[0] + part[1], part[0] - part[1]
        s1, d1 = part[2] + part[3], part[2] - part[3]
        for q, value in enumerate((s0 + s1, d0 + d1, s0 - s1, d0 - d1)):
            high, low = pieces(value, 2)
            lhs[q, :, :block] = high
            lhs[q, :, block:] = low
        for q in range(4):
            high, low = lhs[q, :, :block], lhs[q, :, block:]
            modes = jnp.dot(high, joint[0, q], preferred_element_type=F32)
            modes = modes + jnp.dot(low, joint[0, q], preferred_element_type=F32)
            modes = modes + jnp.dot(high, joint[1, q], preferred_element_type=F32)
            spectrum[:, :, q * block : (q + 1) * block] = modes.reshape(points, pairs, block)

        @pl.when(step < n_pair - 1)
        def _():
            later = order(step + 1)
            move(orb_ref, later, 0, me ^ (later * meets)).wait_recv()
            for m in range(1, meets):
                move(held.at[later, 0], later, m, me ^ m).start()

        @pl.when(step == 3)
        def _():
            for x in range(1, n_pair):
                pltpu.make_async_remote_copy(
                    src_ref=sums, dst_ref=pair_in.at[x], send_sem=pair_send.at[x], recv_sem=pair_recv.at[x],
                    device_id={"pair": group ^ x}, device_id_type=MESH,
                ).start()

        for t in range(plane // 128):
            y, z = convolve(base, t)
            for j in range(planes):
                field[j, :, t * 128 : (t + 1) * 128] = z[j]

        occ_b = jnp.zeros((pairs, 128), F32)
        occ_a = jnp.zeros((pairs, 128), F32)
        for m in range(meets):
            partner = me ^ (chunk * meets + m)
            for b in range(per_owner):
                weight = occ_ref[partner * per_owner + b]
                occ_b = jnp.where(lax.rem(sub, per_a) == m * per_owner + b, weight, occ_b)
        for a in range(per_owner):
            occ_a = jnp.where(sub // per_a == a, occ_ref[me * per_owner + a], occ_a)

        @pl.when(chunk == group)
        def _():
            def more(h, acc):
                start = lax.rem(base + h * planes, points)
                for t in range(plane // 128):
                    y, z = convolve(start, t)
                    for j in range(planes):
                        acc = acc + y[j] * z[j]
                return acc

            acc = lax.fori_loop(0, n_pair, more, jnp.zeros((pairs, 128), F32))
            tile[...] = acc * occ_a * occ_b

        z = field[...].reshape(planes * pairs, plane)
        back = []
        for q in range(4):
            high, low = pieces(z[:, q * block : (q + 1) * block], 2)
            value = lax.dot_general(high, joint[0, q], (((1,), (1,)), ((), ())), preferred_element_type=F32)
            value = value + lax.dot_general(low, joint[0, q], (((1,), (1,)), ((), ())), preferred_element_type=F32)
            value = value + lax.dot_general(high, joint[1, q], (((1,), (1,)), ((), ())), preferred_element_type=F32)
            back.append(value)
        s0, d0 = back[0] + back[1], back[0] - back[1]
        s1, d1 = back[2] + back[3], back[2] - back[3]
        scale = jnp.concatenate([occ_b] * (block // 128), axis=1)[None]
        for q, value in enumerate((s0 + s1, d0 + d1, s0 - s1, d0 - d1)):
            cut = slice(q * block, (q + 1) * block)
            potential = value.reshape(planes, pairs, block)
            total[:, :, cut] += potential * (right[pl.ds(base, planes), :, cut] * scale)

        @pl.when(step == 2)
        def _():
            acc = tile[...]
            for x in range(1, n_band):
                pltpu.make_async_remote_copy(
                    src_ref=tile, dst_ref=band_in.at[x], send_sem=band_send.at[x], recv_sem=band_recv.at[x],
                    device_id={"band": me ^ x}, device_id_type=MESH,
                ).wait()
                acc = acc + band_in[x]
            sums[...] = acc

        return carry

    lax.fori_loop(0, n_pair, step_body, 0)

    for a in range(per_owner):
        value = total[:, a * per_a, :]
        for o in range(1, per_a):
            value = value + total[:, a * per_a + o, :]
        for v in range(2):
            result = 0.0
            for term in pieces(value[:, v * 2 * block : (v + 1) * 2 * block], 3):
                result = result + lax.dot_general(
                    term, maps[v], (((1,), (1,)), ((), ())), preferred_element_type=F32
                )
            out_ref[a, :, v * 2 * block : (v + 1) * 2 * block] = -result

    for x in range(1, n_pair):
        pltpu.make_async_remote_copy(
            src_ref=sums, dst_ref=pair_in.at[x], send_sem=pair_send.at[x], recv_sem=pair_recv.at[x],
            device_id={"pair": group ^ x}, device_id_type=MESH,
        ).wait()
    member = lax.rem(sub, per_a) // per_owner
    for s in range(meets):
        wanted = plan_ref[group * meets + s]
        acc = jnp.zeros((pairs, 128), F32)
        for x in range(n_pair):
            value = sums[...] if x == 0 else pair_in[x]
            acc = acc + jnp.where((group ^ x) * meets + member == wanted, value, 0.0)
        slot_ref[s] = -jnp.sum(acc) * (1.0 / (2.0 * n_band * per_owner * points**3))

    for m in range(1, meets):
        move(orb_ref, 0, m, me ^ m).wait_send()

    def drain(step, carry):
        chunk = order(step)
        move(orb_ref, chunk, 0, me ^ (chunk * meets)).wait_send()
        for m in range(1, meets):
            move(held.at[chunk, 0], chunk, m, me ^ m).wait_send()
        return carry

    lax.fori_loop(1, n_pair, drain, 0)


def solution(mesh):
    n_band, n_pair = mesh.shape["band"], mesh.shape["pair"]
    meets = n_band // n_pair

    def on_device(orbitals, ker, occupations, plan):
        per_owner, points, plane = orbitals.shape
        planes = points // n_pair
        pairs = per_owner * per_owner * meets
        block = plane // 4
        maps, joint, cosine = tables(points)
        vmem = pl.BlockSpec(memory_space=pltpu.VMEM)
        smem = pl.BlockSpec(memory_space=pltpu.SMEM)
        anyw = pl.BlockSpec(memory_space=pl.ANY)
        dma = pltpu.SemaphoreType.DMA
        return pl.pallas_call(
            functools.partial(kernel, (n_band, n_pair, points, per_owner)),
            out_shape=(
                jax.ShapeDtypeStruct((per_owner, planes, plane), F32),
                jax.ShapeDtypeStruct((meets,), F32),
            ),
            in_specs=[smem, smem, vmem, vmem, vmem, anyw, anyw],
            out_specs=(vmem, smem),
            scratch_shapes=[
                pltpu.VMEM((n_pair, meets, per_owner, points, plane), BF16),
                pltpu.VMEM(maps.shape, BF16),
                pltpu.VMEM(joint.shape, BF16),
                pltpu.VMEM((points, pairs, plane), F32),
                pltpu.VMEM((points, pairs, plane), F32),
                pltpu.VMEM((points // 2 + 1, 8, plane), F32),
                pltpu.VMEM((4, points * pairs, 2 * block), BF16),
                pltpu.VMEM((points, pairs, plane), F32),
                pltpu.VMEM((planes, pairs, plane), F32),
                pltpu.VMEM((planes, pairs, plane), F32),
                pltpu.VMEM((pairs, 128), F32),
                pltpu.VMEM((pairs, 128), F32),
                pltpu.VMEM((n_band, pairs, 128), F32),
                pltpu.VMEM((n_pair, pairs, 128), F32),
                dma((2,)),
                dma((n_pair, meets)),
                dma((n_pair, meets)),
                dma((n_band,)),
                dma((n_band,)),
                dma((n_pair,)),
                dma((n_pair,)),
            ],
            compiler_params=pltpu.CompilerParams(
                collective_id=0, has_side_effects=True, vmem_limit_bytes=48 * 1024 * 1024
            ),
        )(plan, occupations, orbitals, ker, jnp.asarray(cosine), jnp.asarray(maps), jnp.asarray(joint))

    return jax.shard_map(
        on_device,
        mesh=mesh,
        in_specs=(P("band", None, None), P(), P(), P()),
        out_specs=(P("band", "pair", None), P("pair")),
        check_vma=False,
    )
```

```python
import functools
import math

import jax
import jax.numpy as jnp
import ml_dtypes
import numpy as np
from jax import lax
from jax.experimental import pallas as pl
from jax.experimental.pallas import tpu as pltpu
from jax.sharding import PartitionSpec as P

MESH = pl.DeviceIdType.MESH
F32 = jnp.float32
BF16 = jnp.bfloat16


def pieces(value, count):
    terms = []
    for at in range(count):
        term = value.astype(BF16)
        terms.append(term)
        if at < count - 1:
            value = value - term.astype(F32)
    return terms


def tables(points):
    half = points // 2
    block = half * half
    sw, row, col = (x.reshape(-1) for x in np.meshgrid(np.arange(2), np.arange(half), np.arange(half), indexing="ij"))
    target = np.arange(2 * block)
    place = np.where(sw == 0, col, points - 1 - col)
    fold = np.zeros((2, 2 * block, 2 * block), np.float32)
    fold[0, row * points + place, target] = 1.0
    fold[1, (half - 1 - row) * points + place, target] = 1.0
    select = np.zeros((2 * block, 2 * block), np.float32)
    select[row * points + col + sw, target] = 1.0
    spot = np.arange(half) + 0.5
    basis = []
    for odd in range(2):
        mode = np.arange(half) + odd
        angle = 2.0 * np.pi * mode[:, None] * spot[None, :] / points
        edge = (mode == 0) | (mode == half)
        factor = np.where(edge, math.sqrt(1.0 / half), math.sqrt(2.0 / half))
        basis.append((np.sin(angle) if odd else np.cos(angle)) * factor[:, None])
    joint = np.stack([np.kron(basis[v], basis[w]).T for v in range(2) for w in range(2)])
    high = joint.astype(ml_dtypes.bfloat16)
    low = (joint - high.astype(np.float64)).astype(ml_dtypes.bfloat16)
    shift = np.arange(-(-(half + 1) // 8) * 8)
    cosine = np.cos(2.0 * np.pi * shift[:, None] * np.arange(points)[None, :] / points) / (4.0 * points)
    maps = np.concatenate([fold, select[None]]).astype(ml_dtypes.bfloat16)
    return maps, np.stack([high, low]), cosine.astype(np.float32)


def kernel(
    dims,
    plan_hbm, occ_hbm, orb_ref, ker_hbm, cos_hbm, maps_hbm, joint_hbm,
    out_ref, slot_ref,
    plan_ref, occ_ref, ker_ref, cos_ref, held, maps, joint, left, right, spread, lhs, spectrum, field, total, tile, sums, band_in, pair_in,
    load_sem, send_sem, recv_sem, band_send, band_recv, pair_send, pair_recv,
):
    n_band, n_pair, points, per_owner = dims
    meets = n_band // n_pair
    plane = points * points
    half = points // 2
    block = half * half
    planes = points // n_pair
    pairs = per_owner * per_owner * meets
    rows = points * pairs
    me = lax.axis_index("band")
    group = lax.axis_index("pair")
    base = group * planes

    wanted_loads = (
        (orb_ref, held.at[0, 0]), (cos_hbm, cos_ref), (ker_hbm, ker_ref), (maps_hbm, maps),
        (joint_hbm, joint), (plan_hbm, plan_ref), (occ_hbm, occ_ref),
    )
    loads = [pltpu.make_async_copy(src, dst, load_sem.at[at]) for at, (src, dst) in enumerate(wanted_loads)]
    for load in loads:
        load.start()

    barrier = pltpu.get_barrier_semaphore()
    for x in range(1, n_band):
        pl.semaphore_signal(barrier, inc=1, device_id={"band": me ^ x}, device_id_type=MESH)
    for x in range(1, n_pair):
        pl.semaphore_signal(barrier, inc=1, device_id={"pair": group ^ x}, device_id_type=MESH)
    pl.semaphore_wait(barrier, n_band + n_pair - 2)

    def order(step):
        first = jnp.maximum(group, 1) - 1
        return jnp.where(step == 0, 0, 1 + lax.rem(first + step - 1 + (n_pair - 1), n_pair - 1))

    def move(src, chunk, member, target):
        return pltpu.make_async_remote_copy(
            src_ref=src,
            dst_ref=held.at[chunk, member],
            send_sem=send_sem.at[chunk, member],
            recv_sem=recv_sem.at[chunk, member],
            device_id={"band": target},
            device_id_type=MESH,
        )

    for m in range(1, meets):
        move(orb_ref, 0, m, me ^ m).start()

    def send_direct(step, carry):
        chunk = order(step)
        move(orb_ref, chunk, 0, me ^ (chunk * meets)).start()
        return carry

    lax.fori_loop(1, n_pair, send_direct, 0)

    total[...] = jnp.zeros_like(total)

    loads[1].wait()
    loads[2].wait()
    mixed = jnp.dot(cos_ref[...], ker_ref[...], precision=lax.Precision.HIGHEST, preferred_element_type=F32)
    shifted = pltpu.roll(mixed, plane - points, 1)
    loads[3].wait()
    for v, source in enumerate((mixed, shifted)):
        picked = 0.0
        for term in pieces(source[:, : 2 * block], 3):
            picked = picked + jnp.dot(term, maps[2], preferred_element_type=F32)
        for s in range(half + 1):
            spread[s, :, v * 2 * block : (v + 1) * 2 * block] = jnp.broadcast_to(
                picked[s : s + 1], (8, 2 * block)
            )

    def folded(raw):
        return [
            jnp.dot(raw[:, v * 2 * block : (v + 1) * 2 * block], maps[v], preferred_element_type=F32)
            for v in range(2)
        ]

    loads[0].wait()
    own = folded(held[0, 0].reshape(per_owner * points, plane))
    per_a = meets * per_owner
    for a in range(per_owner):
        for v in range(2):
            value = own[v][a * points : (a + 1) * points]
            for o in range(per_a):
                left[:, a * per_a + o, v * 2 * block : (v + 1) * 2 * block] = value
    for load in loads[4:]:
        load.wait()

    sub = lax.broadcasted_iota(jnp.int32, (pairs, 128), 0)

    def convolve(start, t):
        lanes = slice(t * 128, (t + 1) * 128)
        y = [spectrum[lax.rem(start + i, points), :, lanes] for i in range(points)]
        z = []
        for j in range(planes):
            value = spread[0, :, lanes] * y[j] + spread[half, :, lanes] * y[(j + half) % points]
            for s in range(1, half):
                value = value + spread[s, :, lanes] * (y[(j + s) % points] + y[(j - s) % points])
            z.append(value)
        return y, z

    def step_body(step, carry):
        chunk = order(step)

        @pl.when(step == 2)
        def _():
            for x in range(1, n_band):
                pltpu.make_async_remote_copy(
                    src_ref=tile, dst_ref=band_in.at[x], send_sem=band_send.at[x], recv_sem=band_recv.at[x],
                    device_id={"band": me ^ x}, device_id_type=MESH,
                ).start()

        for m in range(1, meets):
            move(orb_ref, chunk, m, me ^ m).wait_recv()
        moved = folded(held[chunk].reshape(meets * per_owner * points, plane))
        for v in range(2):
            for o in range(per_a):
                value = moved[v][o * points : (o + 1) * points]
                for a in range(per_owner):
                    right[:, a * per_a + o, v * 2 * block : (v + 1) * 2 * block] = value

        density = (left[...] * right[...]).reshape(rows, plane)
        part = [density[:, q * block : (q + 1) * block] for q in range(4)]
        s0, d0 = part[0] + part[1], part[0] - part[1]
        s1, d1 = part[2] + part[3], part[2] - part[3]
        for q, value in enumerate((s0 + s1, d0 + d1, s0 - s1, d0 - d1)):
            high, low = pieces(value, 2)
            lhs[q, :, :block] = high
            lhs[q, :, block:] = low
        for q in range(4):
            high, low = lhs[q, :, :block], lhs[q, :, block:]
            modes = jnp.dot(high, joint[0, q], preferred_element_type=F32)
            modes = modes + jnp.dot(low, joint[0, q], preferred_element_type=F32)
            modes = modes + jnp.dot(high, joint[1, q], preferred_element_type=F32)
            spectrum[:, :, q * block : (q + 1) * block] = modes.reshape(points, pairs, block)

        @pl.when(step < n_pair - 1)
        def _():
            later = order(step + 1)
            move(orb_ref, later, 0, me ^ (later * meets)).wait_recv()
            for m in range(1, meets):
                move(held.at[later, 0], later, m, me ^ m).start()

        @pl.when(step == 3)
        def _():
            for x in range(1, n_pair):
                pltpu.make_async_remote_copy(
                    src_ref=sums, dst_ref=pair_in.at[x], send_sem=pair_send.at[x], recv_sem=pair_recv.at[x],
                    device_id={"pair": group ^ x}, device_id_type=MESH,
                ).start()

        for t in range(plane // 128):
            y, z = convolve(base, t)
            for j in range(planes):
                field[j, :, t * 128 : (t + 1) * 128] = z[j]

        occ_b = jnp.zeros((pairs, 128), F32)
        occ_a = jnp.zeros((pairs, 128), F32)
        for m in range(meets):
            partner = me ^ (chunk * meets + m)
            for b in range(per_owner):
                weight = occ_ref[partner * per_owner + b]
                occ_b = jnp.where(lax.rem(sub, per_a) == m * per_owner + b, weight, occ_b)
        for a in range(per_owner):
            occ_a = jnp.where(sub // per_a == a, occ_ref[me * per_owner + a], occ_a)

        @pl.when(chunk == group)
        def _():
            def more(h, acc):
                start = lax.rem(base + h * planes, points)
                for t in range(plane // 128):
                    y, z = convolve(start, t)
                    for j in range(planes):
                        acc = acc + y[j] * z[j]
                return acc

            acc = lax.fori_loop(0, n_pair, more, jnp.zeros((pairs, 128), F32))
            tile[...] = acc * occ_a * occ_b

        z = field[...].reshape(planes * pairs, plane)
        back = []
        for q in range(4):
            high, low = pieces(z[:, q * block : (q + 1) * block], 2)
            value = lax.dot_general(high, joint[0, q], (((1,), (1,)), ((), ())), preferred_element_type=F32)
            value = value + lax.dot_general(low, joint[0, q], (((1,), (1,)), ((), ())), preferred_element_type=F32)
            value = value + lax.dot_general(high, joint[1, q], (((1,), (1,)), ((), ())), preferred_element_type=F32)
            back.append(value)
        s0, d0 = back[0] + back[1], back[0] - back[1]
        s1, d1 = back[2] + back[3], back[2] - back[3]
        scale = jnp.concatenate([occ_b] * (block // 128), axis=1)[None]
        for q, value in enumerate((s0 + s1, d0 + d1, s0 - s1, d0 - d1)):
            cut = slice(q * block, (q + 1) * block)
            potential = value.reshape(planes, pairs, block)
            total[:, :, cut] += potential * (right[pl.ds(base, planes), :, cut] * scale)

        @pl.when(step == 2)
        def _():
            acc = tile[...]
            for x in range(1, n_band):
                pltpu.make_async_remote_copy(
                    src_ref=tile, dst_ref=band_in.at[x], send_sem=band_send.at[x], recv_sem=band_recv.at[x],
                    device_id={"band": me ^ x}, device_id_type=MESH,
                ).wait()
                acc = acc + band_in[x]
            sums[...] = acc

        return carry

    lax.fori_loop(0, n_pair, step_body, 0)

    for a in range(per_owner):
        value = total[:, a * per_a, :]
        for o in range(1, per_a):
            value = value + total[:, a * per_a + o, :]
        for v in range(2):
            result = 0.0
            for term in pieces(value[:, v * 2 * block : (v + 1) * 2 * block], 3):
                result = result + lax.dot_general(
                    term, maps[v], (((1,), (1,)), ((), ())), preferred_element_type=F32
                )
            out_ref[a, :, v * 2 * block : (v + 1) * 2 * block] = -result

    for x in range(1, n_pair):
        pltpu.make_async_remote_copy(
            src_ref=sums, dst_ref=pair_in.at[x], send_sem=pair_send.at[x], recv_sem=pair_recv.at[x],
            device_id={"pair": group ^ x}, device_id_type=MESH,
        ).wait()
    member = lax.rem(sub, per_a) // per_owner
    for s in range(meets):
        wanted = plan_ref[group * meets + s]
        acc = jnp.zeros((pairs, 128), F32)
        for x in range(n_pair):
            value = sums[...] if x == 0 else pair_in[x]
            acc = acc + jnp.where((group ^ x) * meets + member == wanted, value, 0.0)
        slot_ref[s] = -jnp.sum(acc) * (1.0 / (2.0 * n_band * per_owner * points**3))

    for m in range(1, meets):
        move(orb_ref, 0, m, me ^ m).wait_send()

    def drain(step, carry):
        chunk = order(step)
        move(orb_ref, chunk, 0, me ^ (chunk * meets)).wait_send()
        for m in range(1, meets):
            move(held.at[chunk, 0], chunk, m, me ^ m).wait_send()
        return carry

    lax.fori_loop(1, n_pair, drain, 0)


def solution(mesh):
    n_band, n_pair = mesh.shape["band"], mesh.shape["pair"]
    meets = n_band // n_pair

    def on_device(orbitals, ker, occupations, plan):
        per_owner, points, plane = orbitals.shape
        planes = points // n_pair
        pairs = per_owner * per_owner * meets
        block = plane // 4
        maps, joint, cosine = tables(points)
        vmem = pl.BlockSpec(memory_space=pltpu.VMEM)
        smem = pl.BlockSpec(memory_space=pltpu.SMEM)
        anyw = pl.BlockSpec(memory_space=pl.ANY)
        dma = pltpu.SemaphoreType.DMA
        return pl.pallas_call(
            functools.partial(kernel, (n_band, n_pair, points, per_owner)),
            out_shape=(
                jax.ShapeDtypeStruct((per_owner, planes, plane), F32),
                jax.ShapeDtypeStruct((meets,), F32),
            ),
            in_specs=[anyw] * 7,
            out_specs=(vmem, smem),
            scratch_shapes=[
                pltpu.SMEM(plan.shape, jnp.int32),
                pltpu.SMEM(occupations.shape, F32),
                pltpu.VMEM(ker.shape, F32),
                pltpu.VMEM(cosine.shape, F32),
                pltpu.VMEM((n_pair, meets, per_owner, points, plane), BF16),
                pltpu.VMEM(maps.shape, BF16),
                pltpu.VMEM(joint.shape, BF16),
                pltpu.VMEM((points, pairs, plane), F32),
                pltpu.VMEM((points, pairs, plane), F32),
                pltpu.VMEM((points // 2 + 1, 8, plane), F32),
                pltpu.VMEM((4, points * pairs, 2 * block), BF16),
                pltpu.VMEM((points, pairs, plane), F32),
                pltpu.VMEM((planes, pairs, plane), F32),
                pltpu.VMEM((planes, pairs, plane), F32),
                pltpu.VMEM((pairs, 128), F32),
                pltpu.VMEM((pairs, 128), F32),
                pltpu.VMEM((n_band, pairs, 128), F32),
                pltpu.VMEM((n_pair, pairs, 128), F32),
                dma((7,)),
                dma((n_pair, meets)),
                dma((n_pair, meets)),
                dma((n_band,)),
                dma((n_band,)),
                dma((n_pair,)),
                dma((n_pair,)),
            ],
            compiler_params=pltpu.CompilerParams(
                collective_id=0, has_side_effects=True, vmem_limit_bytes=67043328
            ),
        )(plan, occupations, orbitals, ker, jnp.asarray(cosine), jnp.asarray(maps), jnp.asarray(joint))

    return jax.shard_map(
        on_device,
        mesh=mesh,
        in_specs=(P("band", None, None), P(), P(), P()),
        out_specs=(P("band", "pair", None), P("pair")),
        check_vma=False,
    )
```

```python
import functools
import math

import jax
import jax.numpy as jnp
import ml_dtypes
import numpy as np
from jax import lax
from jax.experimental import pallas as pl
from jax.experimental.pallas import tpu as pltpu
from jax.sharding import PartitionSpec as P

MESH = pl.DeviceIdType.MESH
F32 = jnp.float32
BF16 = jnp.bfloat16


def pieces(value, count):
    terms = []
    for at in range(count):
        term = value.astype(BF16)
        terms.append(term)
        if at < count - 1:
            value = value - term.astype(F32)
    return terms


def tables(points, planes):
    half = points // 2
    block = half * half
    sw, row, col = (x.reshape(-1) for x in np.meshgrid(np.arange(2), np.arange(half), np.arange(half), indexing="ij"))
    target = np.arange(2 * block)
    place = np.where(sw == 0, col, points - 1 - col)
    fold = np.zeros((2, 2 * block, 2 * block), np.float32)
    fold[0, row * points + place, target] = 1.0
    fold[1, (half - 1 - row) * points + place, target] = 1.0
    select = np.zeros((2 * block, 2 * block), np.float32)
    select[row * points + col + sw, target] = 1.0
    spot = np.arange(half) + 0.5
    basis = []
    for odd in range(2):
        mode = np.arange(half) + odd
        angle = 2.0 * np.pi * mode[:, None] * spot[None, :] / points
        edge = (mode == 0) | (mode == half)
        factor = np.where(edge, math.sqrt(1.0 / half), math.sqrt(2.0 / half))
        basis.append((np.sin(angle) if odd else np.cos(angle)) * factor[:, None])
    joint = np.stack([np.kron(basis[v], basis[w]).T for v in range(2) for w in range(2)])
    high = joint.astype(ml_dtypes.bfloat16)
    low = (joint - high.astype(np.float64)).astype(ml_dtypes.bfloat16)
    out = np.arange(planes // 2)[:, None, None]
    into = np.arange(half)[None, :, None]
    wave = 2.0 * np.pi * np.arange(points)[None, None, :] / points
    near, far = np.cos(wave * (out - into)), np.cos(wave * (out + into + 1))
    cosine = np.stack([near + far, near - far]).reshape(-1, points) / (8.0 * points)
    maps = np.concatenate([fold, select[None]]).astype(ml_dtypes.bfloat16)
    return maps, np.stack([high, low]), cosine.astype(np.float32)


def kernel(
    dims,
    plan_hbm, occ_hbm, orb_ref, ker_hbm, cos_hbm, maps_hbm, joint_hbm,
    out_ref, slot_ref,
    plan_ref, occ_ref, ker_ref, cos_ref, raw, held, maps, joint, left, right, spread, lhs, spectrum, field,
    partner_part, total, energy, tile, sums, band_in, pair_in,
    load_sem, send_sem, recv_sem, band_send, band_recv, pair_send, pair_recv,
):
    n_band, n_pair, points, per_owner = dims
    meets = n_band // n_pair
    plane = points * points
    half = points // 2
    block = half * half
    planes = points // n_pair
    pairs = per_owner * per_owner * meets
    rows = points * pairs
    me = lax.axis_index("band")
    group = lax.axis_index("pair")
    base = group * planes

    wanted_loads = (
        (orb_ref, raw), (maps_hbm, maps), (ker_hbm, ker_ref), (cos_hbm, cos_ref),
        (joint_hbm, joint), (plan_hbm, plan_ref), (occ_hbm, occ_ref),
    )
    loads = [pltpu.make_async_copy(src, dst, load_sem.at[at]) for at, (src, dst) in enumerate(wanted_loads)]
    for load in loads:
        load.start()

    barrier = pltpu.get_barrier_semaphore()
    for x in range(1, n_band):
        pl.semaphore_signal(barrier, inc=1, device_id={"band": me ^ x}, device_id_type=MESH)
    for x in range(1, n_pair):
        pl.semaphore_signal(barrier, inc=1, device_id={"pair": group ^ x}, device_id_type=MESH)

    loads[0].wait()
    loads[1].wait()
    per_a = meets * per_owner
    for v in range(2):
        cut = slice(v * 2 * block, (v + 1) * 2 * block)
        own = jnp.dot(raw[...].reshape(per_owner * points, plane)[:, cut], maps[v], preferred_element_type=F32)
        held[0, 0, :, :, cut] = own.astype(BF16).reshape(per_owner, points, 2 * block)
        for a in range(per_owner):
            for o in range(per_a):
                left[:, a * per_a + o, cut] = own[a * points : (a + 1) * points]
    tile[...] = jnp.zeros_like(tile)
    pl.semaphore_wait(barrier, n_band + n_pair - 2)

    def order(step):
        first = jnp.maximum(group, 1) - 1
        return jnp.where(step == 0, 0, 1 + lax.rem(first + step - 1 + (n_pair - 1), n_pair - 1))

    mine = held.at[0, 0]

    def move(src, chunk, member, target):
        return pltpu.make_async_remote_copy(
            src_ref=src,
            dst_ref=held.at[chunk, member],
            send_sem=send_sem.at[chunk, member],
            recv_sem=recv_sem.at[chunk, member],
            device_id={"band": target},
            device_id_type=MESH,
        )

    for m in range(1, meets):
        move(mine, 0, m, me ^ m).start()

    def send_direct(step, carry):
        chunk = order(step)
        move(mine, chunk, 0, me ^ (chunk * meets)).start()
        return carry

    lax.fori_loop(1, n_pair, send_direct, 0)

    loads[2].wait()
    loads[3].wait()
    mixed = jnp.dot(cos_ref[...], ker_ref[...], precision=lax.Precision.HIGHEST, preferred_element_type=F32)
    shifted = pltpu.roll(mixed, plane - points, 1)
    for v, source in enumerate((mixed, shifted)):
        picked = 0.0
        for term in pieces(source[:, : 2 * block], 3):
            picked = picked + jnp.dot(term, maps[2], preferred_element_type=F32)
        spread[:, v * 2 * block : (v + 1) * 2 * block] = picked
    for load in loads[4:]:
        load.wait()

    sub = lax.broadcasted_iota(jnp.int32, (pairs, 128), 0)
    member = lax.rem(sub, per_a) // per_owner
    slot_row = lax.broadcasted_iota(jnp.int32, (n_band, 128), 0)
    centre = planes // 2

    def convolve(start, t):
        lanes = slice(t * 128, (t + 1) * 128)
        even, odd = [], []
        for r in range(half):
            upper = spectrum[lax.rem(start + centre + r, points), :, lanes]
            lower = spectrum[lax.rem(start + centre - 1 - r + points, points), :, lanes]
            even.append(upper + lower)
            odd.append(upper - lower)
        result = []
        for kind, values in enumerate((even, odd)):
            for q in range(centre):
                at = (kind * centre + q) * half
                value = jnp.broadcast_to(spread[at : at + 1, lanes], (pairs, 128)) * values[0]
                for r in range(1, half):
                    value = value + jnp.broadcast_to(spread[at + r : at + r + 1, lanes], (pairs, 128)) * values[r]
                result.append(value)
        return even, odd, result

    def add_energy(acc, even, odd, result):
        for q in range(centre):
            acc = acc + even[q] * result[q] + odd[q] * result[centre + q]
        return acc

    def pair_copy(x):
        return pltpu.make_async_remote_copy(
            src_ref=tile, dst_ref=pair_in.at[x], send_sem=pair_send.at[x], recv_sem=pair_recv.at[x],
            device_id={"pair": group ^ x}, device_id_type=MESH,
        )

    def band_copy(x):
        return pltpu.make_async_remote_copy(
            src_ref=sums, dst_ref=band_in.at[x], send_sem=band_send.at[x], recv_sem=band_recv.at[x],
            device_id={"band": me ^ x}, device_id_type=MESH,
        )

    extra_step = jnp.where(group == 0, n_pair - 3, jnp.where(group == n_pair - 1, 1, n_pair - 2))
    extra_block = jnp.where(
        group == 0, n_pair - 2, jnp.where(group == n_pair - 1, 0, jnp.where(group == 1, n_pair - 1, group - 1))
    )

    def step_body(step, carry):
        chunk = order(step)

        @pl.when(step == n_pair - 1)
        def _():
            for x in range(1, n_pair):
                pair_copy(x).start()

        for m in range(1, meets):
            move(mine, chunk, m, me ^ m).wait_recv()
        for o in range(per_a):
            value = held[chunk, o // per_owner, o % per_owner].astype(F32)
            for a in range(per_owner):
                right[:, a * per_a + o, :] = value

        for u in range(0, points, 2):
            density = (left[u : u + 2] * right[u : u + 2]).reshape(2 * pairs, plane)
            part = [density[:, q * block : (q + 1) * block] for q in range(4)]
            s0, d0 = part[0] + part[1], part[0] - part[1]
            s1, d1 = part[2] + part[3], part[2] - part[3]
            for q, value in enumerate((s0 + s1, d0 + d1, s0 - s1, d0 - d1)):
                high, low = pieces(value, 2)
                lhs[q, u * pairs : (u + 2) * pairs, :block] = high
                lhs[q, u * pairs : (u + 2) * pairs, block:] = low
        for q in range(4):
            high, low = lhs[q, :, :block], lhs[q, :, block:]
            modes = jnp.dot(high, joint[0, q], preferred_element_type=F32)
            modes = modes + jnp.dot(low, joint[0, q], preferred_element_type=F32)
            modes = modes + jnp.dot(high, joint[1, q], preferred_element_type=F32)
            spectrum[:, :, q * block : (q + 1) * block] = modes.reshape(points, pairs, block)

        @pl.when(step < n_pair - 1)
        def _():
            later = order(step + 1)
            move(mine, later, 0, me ^ (later * meets)).wait_recv()
            for m in range(1, meets):
                move(held.at[later, 0], later, m, me ^ m).start()

        acc = jnp.zeros((pairs, 128), F32)
        for t in range(plane // 128):
            even, odd, result = convolve(base, t)
            acc = add_energy(acc, even, odd, result)
            for q in range(centre):
                field[step, centre + q, :, t * 128 : (t + 1) * 128] = result[q] + result[centre + q]
                field[step, centre - 1 - q, :, t * 128 : (t + 1) * 128] = result[q] - result[centre + q]
        energy[...] = acc

        @pl.when(step == extra_step)
        def _():
            acc = energy[...]
            for t in range(plane // 128):
                acc = add_energy(acc, *convolve(extra_block * planes, t))
            energy[...] = acc

        occ_b = jnp.zeros((pairs, 128), F32)
        occ_a = jnp.zeros((pairs, 128), F32)
        for m in range(meets):
            partner = me ^ (chunk * meets + m)
            for b in range(per_owner):
                weight = occ_ref[partner * per_owner + b]
                occ_b = jnp.where(lax.rem(sub, per_a) == m * per_owner + b, weight, occ_b)
        for a in range(per_owner):
            occ_a = jnp.where(sub // per_a == a, occ_ref[me * per_owner + a], occ_a)

        @pl.when(step < n_pair - 1)
        def _():
            share = energy[...] * occ_a * occ_b
            for m in range(meets):
                row = jnp.sum(jnp.where(member == m, share, 0.0), axis=0, keepdims=True)
                tile[...] += jnp.where(slot_row == chunk * meets + m, row, 0.0)

        scale = jnp.concatenate([occ_b] * (plane // 128), axis=1)[None]
        partner_part[step] = right[pl.ds(base, planes)] * scale
        return carry

    lax.fori_loop(0, n_pair, step_body, 0)

    across = (((1,), (1,)), ((), ()))
    back = n_pair * planes * pairs
    for q in range(4):
        cut = slice(q * block, (q + 1) * block)
        high, low = pieces(field[:, :, :, cut].reshape(back, block), 2)
        value = lax.dot_general(high, joint[0, q], across, preferred_element_type=F32)
        value = value + lax.dot_general(low, joint[0, q], across, preferred_element_type=F32)
        value = value + lax.dot_general(high, joint[1, q], across, preferred_element_type=F32)
        spectrum[:, :, cut] = value.reshape(points, pairs, block)

    acc = tile[...]
    for x in range(1, n_pair):
        pair_copy(x).wait()
        acc = acc + pair_in[x]
    sums[...] = acc

    for j in range(planes):
        acc = [0.0] * 4
        for step in range(n_pair):
            part = [spectrum[step * planes + j, :, q * block : (q + 1) * block] for q in range(4)]
            s0, d0 = part[0] + part[1], part[0] - part[1]
            s1, d1 = part[2] + part[3], part[2] - part[3]
            for q, value in enumerate((s0 + s1, d0 + d1, s0 - s1, d0 - d1)):
                acc[q] = acc[q] + value * partner_part[step, j, :, q * block : (q + 1) * block]
        for q in range(4):
            total[j, :, q * block : (q + 1) * block] = acc[q]

    for x in range(1, n_band):
        band_copy(x).start()

    stack = []
    for a in range(per_owner):
        value = total[:, a * per_a, :]
        for o in range(1, per_a):
            value = value + total[:, a * per_a + o, :]
        stack.append(value)
    terms = pieces(jnp.concatenate(stack, axis=0), 3)
    for v in range(2):
        cut = slice(v * 2 * block, (v + 1) * 2 * block)
        result = 0.0
        for term in terms:
            result = result + lax.dot_general(term[:, cut], maps[v], across, preferred_element_type=F32)
        out_ref[:, :, cut] = -result.reshape(per_owner, planes, 2 * block)

    acc = sums[...]
    for x in range(1, n_band):
        band_copy(x).wait()
        acc = acc + band_in[x]
    for s in range(meets):
        wanted = plan_ref[group * meets + s]
        value = jnp.sum(jnp.where(slot_row == wanted, acc, 0.0))
        slot_ref[s] = -value * (1.0 / (2.0 * n_band * per_owner * points**3))

    for m in range(1, meets):
        move(mine, 0, m, me ^ m).wait_send()

    def drain(step, carry):
        chunk = order(step)
        move(mine, chunk, 0, me ^ (chunk * meets)).wait_send()
        for m in range(1, meets):
            move(held.at[chunk, 0], chunk, m, me ^ m).wait_send()
        return carry

    lax.fori_loop(1, n_pair, drain, 0)


def solution(mesh):
    n_band, n_pair = mesh.shape["band"], mesh.shape["pair"]
    meets = n_band // n_pair

    def on_device(orbitals, ker, occupations, plan):
        per_owner, points, plane = orbitals.shape
        planes = points // n_pair
        pairs = per_owner * per_owner * meets
        block = plane // 4
        maps, joint, cosine = tables(points, planes)
        vmem = pl.BlockSpec(memory_space=pltpu.VMEM)
        smem = pl.BlockSpec(memory_space=pltpu.SMEM)
        anyw = pl.BlockSpec(memory_space=pl.ANY)
        dma = pltpu.SemaphoreType.DMA
        return pl.pallas_call(
            functools.partial(kernel, (n_band, n_pair, points, per_owner)),
            out_shape=(
                jax.ShapeDtypeStruct((per_owner, planes, plane), F32),
                jax.ShapeDtypeStruct((meets,), F32),
            ),
            in_specs=[anyw] * 7,
            out_specs=(vmem, smem),
            scratch_shapes=[
                pltpu.SMEM(plan.shape, jnp.int32),
                pltpu.SMEM(occupations.shape, F32),
                pltpu.VMEM(ker.shape, F32),
                pltpu.VMEM(cosine.shape, F32),
                pltpu.VMEM(orbitals.shape, BF16),
                pltpu.VMEM((n_pair, meets, per_owner, points, plane), BF16),
                pltpu.VMEM(maps.shape, BF16),
                pltpu.VMEM(joint.shape, BF16),
                pltpu.VMEM((points, pairs, plane), F32),
                pltpu.VMEM((points, pairs, plane), F32),
                pltpu.VMEM((cosine.shape[0], plane), F32),
                pltpu.VMEM((4, points * pairs, 2 * block), BF16),
                pltpu.VMEM((points, pairs, plane), F32),
                pltpu.VMEM((n_pair, planes, pairs, plane), F32),
                pltpu.VMEM((n_pair, planes, pairs, plane), F32),
                pltpu.VMEM((planes, pairs, plane), F32),
                pltpu.VMEM((pairs, 128), F32),
                pltpu.VMEM((n_band, 128), F32),
                pltpu.VMEM((n_band, 128), F32),
                pltpu.VMEM((n_band, n_band, 128), F32),
                pltpu.VMEM((n_pair, n_band, 128), F32),
                dma((7,)),
                dma((n_pair, meets)),
                dma((n_pair, meets)),
                dma((n_band,)),
                dma((n_band,)),
                dma((n_pair,)),
                dma((n_pair,)),
            ],
            compiler_params=pltpu.CompilerParams(
                collective_id=0, has_side_effects=True, vmem_limit_bytes=67043328
            ),
        )(plan, occupations, orbitals, ker, jnp.asarray(cosine), jnp.asarray(maps), jnp.asarray(joint))

    return jax.shard_map(
        on_device,
        mesh=mesh,
        in_specs=(P("band", None, None), P(), P(), P()),
        out_specs=(P("band", "pair", None), P("pair")),
        check_vma=False,
    )
```

```python
import functools
import math

import jax
import jax.numpy as jnp
import ml_dtypes
import numpy as np
from jax import lax
from jax.experimental import pallas as pl
from jax.experimental.pallas import tpu as pltpu
from jax.sharding import PartitionSpec as P

MESH = pl.DeviceIdType.MESH
F32 = jnp.float32
BF16 = jnp.bfloat16


def pieces(value, count):
    terms = []
    for at in range(count):
        term = value.astype(BF16)
        terms.append(term)
        if at < count - 1:
            value = value - term.astype(F32)
    return terms


def tables(points, planes):
    half = points // 2
    block = half * half
    sw, row, col = (x.reshape(-1) for x in np.meshgrid(np.arange(2), np.arange(half), np.arange(half), indexing="ij"))
    target = np.arange(2 * block)
    place = np.where(sw == 0, col, points - 1 - col)
    fold = np.zeros((2, 2 * block, 2 * block), np.float32)
    fold[0, row * points + place, target] = 1.0
    fold[1, (half - 1 - row) * points + place, target] = 1.0
    select = np.zeros((2 * block, 2 * block), np.float32)
    select[row * points + col + sw, target] = 1.0
    spot = np.arange(half) + 0.5
    basis = []
    for odd in range(2):
        mode = np.arange(half) + odd
        angle = 2.0 * np.pi * mode[:, None] * spot[None, :] / points
        edge = (mode == 0) | (mode == half)
        factor = np.where(edge, math.sqrt(1.0 / half), math.sqrt(2.0 / half))
        basis.append((np.sin(angle) if odd else np.cos(angle)) * factor[:, None])
    joint = np.stack([np.kron(basis[v], basis[w]).T for v in range(2) for w in range(2)])
    high = joint.astype(ml_dtypes.bfloat16)
    low = (joint - high.astype(np.float64)).astype(ml_dtypes.bfloat16)
    out = np.arange(planes // 2)[:, None, None]
    into = np.arange(half)[None, :, None]
    wave = 2.0 * np.pi * np.arange(points)[None, None, :] / points
    near, far = np.cos(wave * (out - into)), np.cos(wave * (out + into + 1))
    cosine = np.stack([near + far, near - far]).reshape(-1, points) / (8.0 * points)
    maps = np.concatenate([fold, select[None]]).astype(ml_dtypes.bfloat16)
    return maps, np.stack([high, low]), cosine.astype(np.float32)


def kernel(
    dims,
    plan_hbm, occ_hbm, orb_ref, ker_hbm, cos_hbm, maps_hbm, joint_hbm,
    out_ref, slot_ref,
    plan_ref, occ_ref, ker_ref, cos_ref, raw, held, maps, joint, left, right, spread, lhs, spectrum, field,
    partner_part, total, energy, tile, sums, band_in, pair_in,
    load_sem, send_sem, recv_sem, band_send, band_recv, pair_send, pair_recv,
):
    n_band, n_pair, points, per_owner = dims
    meets = n_band // n_pair
    plane = points * points
    half = points // 2
    block = half * half
    planes = points // n_pair
    pairs = per_owner * per_owner * meets
    rows = points * pairs
    me = lax.axis_index("band")
    group = lax.axis_index("pair")
    base = group * planes

    wanted_loads = (
        (orb_ref, raw), (maps_hbm, maps), (ker_hbm, ker_ref), (cos_hbm, cos_ref),
        (joint_hbm, joint), (plan_hbm, plan_ref), (occ_hbm, occ_ref),
    )
    loads = [pltpu.make_async_copy(src, dst, load_sem.at[at]) for at, (src, dst) in enumerate(wanted_loads)]
    for load in loads:
        load.start()

    barrier = pltpu.get_barrier_semaphore()
    for x in range(1, n_band):
        pl.semaphore_signal(barrier, inc=1, device_id={"band": me ^ x}, device_id_type=MESH)
    for x in range(1, n_pair):
        pl.semaphore_signal(barrier, inc=1, device_id={"pair": group ^ x}, device_id_type=MESH)

    loads[0].wait()
    loads[1].wait()
    per_a = meets * per_owner
    for v in range(2):
        cut = slice(v * 2 * block, (v + 1) * 2 * block)
        own = jnp.dot(raw[...].reshape(per_owner * points, plane)[:, cut], maps[v], preferred_element_type=F32)
        held[0, 0, :, :, cut] = own.astype(BF16).reshape(per_owner, points, 2 * block)
        for a in range(per_owner):
            for o in range(per_a):
                left[:, a * per_a + o, cut] = own[a * points : (a + 1) * points]
    tile[...] = jnp.zeros_like(tile)
    pl.semaphore_wait(barrier, n_band + n_pair - 2)

    def order(step):
        first = jnp.maximum(group, 1) - 1
        return jnp.where(step == 0, 0, 1 + lax.rem(first + step - 1 + (n_pair - 1), n_pair - 1))

    mine = held.at[0, 0]

    def move(src, chunk, member, target):
        return pltpu.make_async_remote_copy(
            src_ref=src,
            dst_ref=held.at[chunk, member],
            send_sem=send_sem.at[chunk, member],
            recv_sem=recv_sem.at[chunk, member],
            device_id={"band": target},
            device_id_type=MESH,
        )

    for m in range(1, meets):
        move(mine, 0, m, me ^ m).start()

    def send_direct(step, carry):
        chunk = order(step)
        move(mine, chunk, 0, me ^ (chunk * meets)).start()
        return carry

    lax.fori_loop(1, n_pair, send_direct, 0)

    loads[2].wait()
    loads[3].wait()
    given = ker_ref[...]
    shifted = pltpu.roll(given, plane - points, 1)
    for v, source in enumerate((given, shifted)):
        picked = 0.0
        for term in pieces(source[:, : 2 * block], 3):
            picked = picked + jnp.dot(term, maps[2], preferred_element_type=F32)
        spread[:, v * 2 * block : (v + 1) * 2 * block] = jnp.dot(
            cos_ref[...], picked, precision=lax.Precision.HIGHEST, preferred_element_type=F32
        )
    for load in loads[4:]:
        load.wait()

    sub = lax.broadcasted_iota(jnp.int32, (pairs, 128), 0)
    member = lax.rem(sub, per_a) // per_owner
    slot_row = lax.broadcasted_iota(jnp.int32, (n_band, 128), 0)
    centre = planes // 2

    def convolve(start, t):
        lanes = slice(t * 128, (t + 1) * 128)
        even, odd = [], []
        for r in range(half):
            upper = spectrum[lax.rem(start + centre + r, points), :, lanes]
            lower = spectrum[lax.rem(start + centre - 1 - r + points, points), :, lanes]
            even.append(upper + lower)
            odd.append(upper - lower)
        result = []
        for kind, values in enumerate((even, odd)):
            for q in range(centre):
                at = (kind * centre + q) * half
                value = jnp.broadcast_to(spread[at : at + 1, lanes], (pairs, 128)) * values[0]
                for r in range(1, half):
                    value = value + jnp.broadcast_to(spread[at + r : at + r + 1, lanes], (pairs, 128)) * values[r]
                result.append(value)
        return even, odd, result

    def add_energy(acc, even, odd, result):
        for q in range(centre):
            acc = acc + even[q] * result[q] + odd[q] * result[centre + q]
        return acc

    def pair_copy(x):
        return pltpu.make_async_remote_copy(
            src_ref=tile, dst_ref=pair_in.at[x], send_sem=pair_send.at[x], recv_sem=pair_recv.at[x],
            device_id={"pair": group ^ x}, device_id_type=MESH,
        )

    def band_copy(x):
        return pltpu.make_async_remote_copy(
            src_ref=sums, dst_ref=band_in.at[x], send_sem=band_send.at[x], recv_sem=band_recv.at[x],
            device_id={"band": me ^ x}, device_id_type=MESH,
        )

    extra_step = jnp.where(group == 0, n_pair - 3, jnp.where(group == n_pair - 1, 1, n_pair - 2))
    extra_block = jnp.where(
        group == 0, n_pair - 2, jnp.where(group == n_pair - 1, 0, jnp.where(group == 1, n_pair - 1, group - 1))
    )

    def step_body(step, carry):
        chunk = order(step)

        @pl.when(step == n_pair - 1)
        def _():
            for x in range(1, n_pair):
                pair_copy(x).start()

        for m in range(1, meets):
            move(mine, chunk, m, me ^ m).wait_recv()
        for o in range(per_a):
            value = held[chunk, o // per_owner, o % per_owner].astype(F32)
            for a in range(per_owner):
                right[:, a * per_a + o, :] = value

        for u in range(0, points, 2):
            density = (left[u : u + 2] * right[u : u + 2]).reshape(2 * pairs, plane)
            part = [density[:, q * block : (q + 1) * block] for q in range(4)]
            s0, d0 = part[0] + part[1], part[0] - part[1]
            s1, d1 = part[2] + part[3], part[2] - part[3]
            for q, value in enumerate((s0 + s1, d0 + d1, s0 - s1, d0 - d1)):
                high, low = pieces(value, 2)
                lhs[q, u * pairs : (u + 2) * pairs, :block] = high
                lhs[q, u * pairs : (u + 2) * pairs, block:] = low
        for q in range(4):
            high, low = lhs[q, :, :block], lhs[q, :, block:]
            modes = jnp.dot(high, joint[0, q], preferred_element_type=F32)
            modes = modes + jnp.dot(low, joint[0, q], preferred_element_type=F32)
            modes = modes + jnp.dot(high, joint[1, q], preferred_element_type=F32)
            spectrum[:, :, q * block : (q + 1) * block] = modes.reshape(points, pairs, block)

        @pl.when(step < n_pair - 1)
        def _():
            later = order(step + 1)
            move(mine, later, 0, me ^ (later * meets)).wait_recv()
            for m in range(1, meets):
                move(held.at[later, 0], later, m, me ^ m).start()

        acc = jnp.zeros((pairs, 128), F32)
        for t in range(plane // 128):
            even, odd, result = convolve(base, t)
            acc = add_energy(acc, even, odd, result)
            for q in range(centre):
                field[step, centre + q, :, t * 128 : (t + 1) * 128] = result[q] + result[centre + q]
                field[step, centre - 1 - q, :, t * 128 : (t + 1) * 128] = result[q] - result[centre + q]
        energy[...] = acc

        @pl.when(step == extra_step)
        def _():
            acc = energy[...]
            for t in range(plane // 128):
                acc = add_energy(acc, *convolve(extra_block * planes, t))
            energy[...] = acc

        occ_b = jnp.zeros((pairs, 128), F32)
        occ_a = jnp.zeros((pairs, 128), F32)
        for m in range(meets):
            partner = me ^ (chunk * meets + m)
            for b in range(per_owner):
                weight = occ_ref[partner * per_owner + b]
                occ_b = jnp.where(lax.rem(sub, per_a) == m * per_owner + b, weight, occ_b)
        for a in range(per_owner):
            occ_a = jnp.where(sub // per_a == a, occ_ref[me * per_owner + a], occ_a)

        @pl.when(step < n_pair - 1)
        def _():
            share = energy[...] * occ_a * occ_b
            for m in range(meets):
                row = jnp.sum(jnp.where(member == m, share, 0.0), axis=0, keepdims=True)
                tile[...] += jnp.where(slot_row == chunk * meets + m, row, 0.0)

        scale = jnp.concatenate([occ_b] * (plane // 128), axis=1)[None]
        partner_part[step] = right[pl.ds(base, planes)] * scale
        return carry

    lax.fori_loop(0, n_pair, step_body, 0)

    across = (((1,), (1,)), ((), ()))
    back = n_pair * planes * pairs
    for q in range(4):
        cut = slice(q * block, (q + 1) * block)
        high, low = pieces(field[:, :, :, cut].reshape(back, block), 2)
        value = lax.dot_general(high, joint[0, q], across, preferred_element_type=F32)
        value = value + lax.dot_general(low, joint[0, q], across, preferred_element_type=F32)
        value = value + lax.dot_general(high, joint[1, q], across, preferred_element_type=F32)
        spectrum[:, :, cut] = value.reshape(points, pairs, block)

    acc = tile[...]
    for x in range(1, n_pair):
        pair_copy(x).wait()
        acc = acc + pair_in[x]
    sums[...] = acc

    for j in range(planes):
        acc = [0.0] * 4
        for step in range(n_pair):
            part = [spectrum[step * planes + j, :, q * block : (q + 1) * block] for q in range(4)]
            s0, d0 = part[0] + part[1], part[0] - part[1]
            s1, d1 = part[2] + part[3], part[2] - part[3]
            for q, value in enumerate((s0 + s1, d0 + d1, s0 - s1, d0 - d1)):
                acc[q] = acc[q] + value * partner_part[step, j, :, q * block : (q + 1) * block]
        for q in range(4):
            total[j, :, q * block : (q + 1) * block] = acc[q]

    for x in range(1, n_band):
        band_copy(x).start()

    stack = []
    for a in range(per_owner):
        value = total[:, a * per_a, :]
        for o in range(1, per_a):
            value = value + total[:, a * per_a + o, :]
        stack.append(value)
    terms = pieces(jnp.concatenate(stack, axis=0), 3)
    for v in range(2):
        cut = slice(v * 2 * block, (v + 1) * 2 * block)
        result = 0.0
        for term in terms:
            result = result + lax.dot_general(term[:, cut], maps[v], across, preferred_element_type=F32)
        out_ref[:, :, cut] = -result.reshape(per_owner, planes, 2 * block)

    acc = sums[...]
    for x in range(1, n_band):
        band_copy(x).wait()
        acc = acc + band_in[x]
    for s in range(meets):
        wanted = plan_ref[group * meets + s]
        value = jnp.sum(jnp.where(slot_row == wanted, acc, 0.0))
        slot_ref[s] = -value * (1.0 / (2.0 * n_band * per_owner * points**3))

    for m in range(1, meets):
        move(mine, 0, m, me ^ m).wait_send()

    def drain(step, carry):
        chunk = order(step)
        move(mine, chunk, 0, me ^ (chunk * meets)).wait_send()
        for m in range(1, meets):
            move(held.at[chunk, 0], chunk, m, me ^ m).wait_send()
        return carry

    lax.fori_loop(1, n_pair, drain, 0)


def solution(mesh):
    n_band, n_pair = mesh.shape["band"], mesh.shape["pair"]
    meets = n_band // n_pair

    def on_device(orbitals, ker, occupations, plan):
        per_owner, points, plane = orbitals.shape
        planes = points // n_pair
        pairs = per_owner * per_owner * meets
        block = plane // 4
        maps, joint, cosine = tables(points, planes)
        vmem = pl.BlockSpec(memory_space=pltpu.VMEM)
        smem = pl.BlockSpec(memory_space=pltpu.SMEM)
        hbm = pl.BlockSpec(memory_space=pltpu.HBM)
        dma = pltpu.SemaphoreType.DMA
        return pl.pallas_call(
            functools.partial(kernel, (n_band, n_pair, points, per_owner)),
            out_shape=(
                jax.ShapeDtypeStruct((per_owner, planes, plane), F32),
                jax.ShapeDtypeStruct((meets,), F32),
            ),
            in_specs=[hbm] * 7,
            out_specs=(vmem, smem),
            scratch_shapes=[
                pltpu.SMEM(plan.shape, jnp.int32),
                pltpu.SMEM(occupations.shape, F32),
                pltpu.VMEM(ker.shape, F32),
                pltpu.VMEM(cosine.shape, F32),
                pltpu.VMEM(orbitals.shape, BF16),
                pltpu.VMEM((n_pair, meets, per_owner, points, plane), BF16),
                pltpu.VMEM(maps.shape, BF16),
                pltpu.VMEM(joint.shape, BF16),
                pltpu.VMEM((points, pairs, plane), F32),
                pltpu.VMEM((points, pairs, plane), F32),
                pltpu.VMEM((cosine.shape[0], plane), F32),
                pltpu.VMEM((4, points * pairs, 2 * block), BF16),
                pltpu.VMEM((points, pairs, plane), F32),
                pltpu.VMEM((n_pair, planes, pairs, plane), F32),
                pltpu.VMEM((n_pair, planes, pairs, plane), F32),
                pltpu.VMEM((planes, pairs, plane), F32),
                pltpu.VMEM((pairs, 128), F32),
                pltpu.VMEM((n_band, 128), F32),
                pltpu.VMEM((n_band, 128), F32),
                pltpu.VMEM((n_band, n_band, 128), F32),
                pltpu.VMEM((n_pair, n_band, 128), F32),
                dma((7,)),
                dma((n_pair, meets)),
                dma((n_pair, meets)),
                dma((n_band,)),
                dma((n_band,)),
                dma((n_pair,)),
                dma((n_pair,)),
            ],
            compiler_params=pltpu.CompilerParams(
                collective_id=0, has_side_effects=True, vmem_limit_bytes=48 * 1024 * 1024
            ),
        )(*(
            pltpu.with_memory_space_constraint(value, pltpu.HBM)
            for value in (plan, occupations, orbitals, ker, jnp.asarray(cosine), jnp.asarray(maps), jnp.asarray(joint))
        ))

    return jax.shard_map(
        on_device,
        mesh=mesh,
        in_specs=(P("band", None, None), P(), P(), P()),
        out_specs=(P("band", "pair", None), P("pair")),
        check_vma=False,
    )
```

```python
import functools
import math

import jax
import jax.numpy as jnp
import ml_dtypes
import numpy as np
from jax import lax
from jax.experimental import pallas as pl
from jax.experimental.pallas import tpu as pltpu
from jax.sharding import PartitionSpec as P

MESH = pl.DeviceIdType.MESH
F32 = jnp.float32
BF16 = jnp.bfloat16


def pieces(value, count):
    terms = []
    for at in range(count):
        term = value.astype(BF16)
        terms.append(term)
        if at < count - 1:
            value = value - term.astype(F32)
    return terms


def tables(points, planes):
    half = points // 2
    block = half * half
    sw, row, col = (x.reshape(-1) for x in np.meshgrid(np.arange(2), np.arange(half), np.arange(half), indexing="ij"))
    target = np.arange(2 * block)
    place = np.where(sw == 0, col, points - 1 - col)
    fold = np.zeros((2, 2 * block, 2 * block), np.float32)
    fold[0, row * points + place, target] = 1.0
    fold[1, (half - 1 - row) * points + place, target] = 1.0
    select = np.zeros((2 * block, 2 * block), np.float32)
    select[row * points + col + sw, target] = 1.0
    spot = np.arange(half) + 0.5
    basis = []
    for odd in range(2):
        mode = np.arange(half) + odd
        angle = 2.0 * np.pi * mode[:, None] * spot[None, :] / points
        edge = (mode == 0) | (mode == half)
        factor = np.where(edge, math.sqrt(1.0 / half), math.sqrt(2.0 / half))
        basis.append((np.sin(angle) if odd else np.cos(angle)) * factor[:, None])
    joint = np.stack([np.kron(basis[v], basis[w]).T for v in range(2) for w in range(2)])
    high = joint.astype(ml_dtypes.bfloat16)
    low = (joint - high.astype(np.float64)).astype(ml_dtypes.bfloat16)
    out = np.arange(planes // 2)[:, None, None]
    into = np.arange(half)[None, :, None]
    wave = 2.0 * np.pi * np.arange(points)[None, None, :] / points
    near, far = np.cos(wave * (out - into)), np.cos(wave * (out + into + 1))
    cosine = np.stack([near + far, near - far]).reshape(-1, points) / (8.0 * points)
    maps = np.concatenate([fold, select[None]]).astype(ml_dtypes.bfloat16)
    return maps, np.stack([high, low]), cosine.astype(np.float32)


def kernel(
    dims,
    plan_hbm, occ_hbm, orb_ref, ker_hbm, cos_hbm, maps_hbm, joint_hbm,
    out_ref, slot_ref,
    plan_ref, occ_ref, ker_ref, cos_ref, raw, held, maps, joint, left, right, spread, lhs, spectrum, field,
    partner_part, total, energy, tile, sums, band_in, pair_in,
    load_sem, send_sem, recv_sem, band_send, band_recv, pair_send, pair_recv,
):
    n_band, n_pair, points, per_owner = dims
    meets = n_band // n_pair
    plane = points * points
    half = points // 2
    block = half * half
    planes = points // n_pair
    pairs = per_owner * per_owner * meets
    rows = points * pairs
    me = lax.axis_index("band")
    group = lax.axis_index("pair")
    base = group * planes

    wanted_loads = (
        (orb_ref, raw), (maps_hbm, maps), (ker_hbm, ker_ref), (cos_hbm, cos_ref),
        (joint_hbm, joint), (plan_hbm, plan_ref), (occ_hbm, occ_ref),
    )
    loads = [pltpu.make_async_copy(src, dst, load_sem.at[at]) for at, (src, dst) in enumerate(wanted_loads)]
    for load in loads:
        load.start()

    barrier = pltpu.get_barrier_semaphore()
    for x in range(1, n_band):
        pl.semaphore_signal(barrier, inc=1, device_id={"band": me ^ x}, device_id_type=MESH)
    for x in range(1, n_pair):
        pl.semaphore_signal(barrier, inc=1, device_id={"pair": group ^ x}, device_id_type=MESH)

    loads[0].wait()
    loads[1].wait()
    per_a = meets * per_owner
    for v in range(2):
        cut = slice(v * 2 * block, (v + 1) * 2 * block)
        own = jnp.dot(raw[...].reshape(per_owner * points, plane)[:, cut], maps[v], preferred_element_type=F32)
        held[0, 0, :, :, cut] = own.astype(BF16).reshape(per_owner, points, 2 * block)
        for a in range(per_owner):
            for o in range(per_a):
                left[:, a * per_a + o, cut] = own[a * points : (a + 1) * points]
    tile[...] = jnp.zeros_like(tile)
    pl.semaphore_wait(barrier, n_band + n_pair - 2)

    def order(step):
        first = jnp.maximum(group, 1) - 1
        return jnp.where(step == 0, 0, 1 + lax.rem(first + step - 1 + (n_pair - 1), n_pair - 1))

    mine = held.at[0, 0]

    def move(src, chunk, member, target):
        return pltpu.make_async_remote_copy(
            src_ref=src,
            dst_ref=held.at[chunk, member],
            send_sem=send_sem.at[chunk, member],
            recv_sem=recv_sem.at[chunk, member],
            device_id={"band": target},
            device_id_type=MESH,
        )

    for m in range(1, meets):
        move(mine, 0, m, me ^ m).start()

    def send_direct(step, carry):
        chunk = order(step)
        move(mine, chunk, 0, me ^ (chunk * meets)).start()
        return carry

    lax.fori_loop(1, n_pair, send_direct, 0)

    loads[2].wait()
    loads[3].wait()
    given = ker_ref[...]
    shifted = pltpu.roll(given, plane - points, 1)
    for v, source in enumerate((given, shifted)):
        parts = jnp.dot(
            jnp.concatenate(pieces(source[:, : 2 * block], 3), axis=0), maps[2], preferred_element_type=F32
        )
        picked = parts[:points] + parts[points : 2 * points] + parts[2 * points :]
        spread[:, v * 2 * block : (v + 1) * 2 * block] = jnp.dot(
            cos_ref[...], picked, precision=lax.Precision.HIGHEST, preferred_element_type=F32
        )
    for load in loads[4:]:
        load.wait()

    sub = lax.broadcasted_iota(jnp.int32, (pairs, 128), 0)
    member = lax.rem(sub, per_a) // per_owner
    slot_row = lax.broadcasted_iota(jnp.int32, (n_band, 128), 0)
    centre = planes // 2

    def convolve(start, t):
        lanes = slice(t * 128, (t + 1) * 128)
        even, odd = [], []
        for r in range(half):
            upper = spectrum[lax.rem(start + centre + r, points), :, lanes]
            lower = spectrum[lax.rem(start + centre - 1 - r + points, points), :, lanes]
            even.append(upper + lower)
            odd.append(upper - lower)
        result = []
        for kind, values in enumerate((even, odd)):
            for q in range(centre):
                at = (kind * centre + q) * half
                value = jnp.broadcast_to(spread[at : at + 1, lanes], (pairs, 128)) * values[0]
                for r in range(1, half):
                    value = value + jnp.broadcast_to(spread[at + r : at + r + 1, lanes], (pairs, 128)) * values[r]
                result.append(value)
        return even, odd, result

    def add_energy(acc, even, odd, result):
        for q in range(centre):
            acc = acc + even[q] * result[q] + odd[q] * result[centre + q]
        return acc

    def pair_copy(x):
        return pltpu.make_async_remote_copy(
            src_ref=tile, dst_ref=pair_in.at[x], send_sem=pair_send.at[x], recv_sem=pair_recv.at[x],
            device_id={"pair": group ^ x}, device_id_type=MESH,
        )

    def band_copy(x):
        return pltpu.make_async_remote_copy(
            src_ref=sums, dst_ref=band_in.at[x], send_sem=band_send.at[x], recv_sem=band_recv.at[x],
            device_id={"band": me ^ x}, device_id_type=MESH,
        )

    extra_step = jnp.where(group == 0, n_pair - 3, jnp.where(group == n_pair - 1, 1, n_pair - 2))
    extra_block = jnp.where(
        group == 0, n_pair - 2, jnp.where(group == n_pair - 1, 0, jnp.where(group == 1, n_pair - 1, group - 1))
    )

    def step_body(step, carry):
        chunk = order(step)

        @pl.when(step == n_pair - 1)
        def _():
            for x in range(1, n_pair):
                pair_copy(x).start()

        for m in range(1, meets):
            move(mine, chunk, m, me ^ m).wait_recv()
        for o in range(per_a):
            value = held[chunk, o // per_owner, o % per_owner].astype(F32)
            for a in range(per_owner):
                right[:, a * per_a + o, :] = value

        for u in range(0, points, 2):
            density = (left[u : u + 2] * right[u : u + 2]).reshape(2 * pairs, plane)
            part = [density[:, q * block : (q + 1) * block] for q in range(4)]
            s0, d0 = part[0] + part[1], part[0] - part[1]
            s1, d1 = part[2] + part[3], part[2] - part[3]
            for q, value in enumerate((s0 + s1, d0 + d1, s0 - s1, d0 - d1)):
                high, low = pieces(value, 2)
                lhs[q, u * pairs : (u + 2) * pairs, :block] = high
                lhs[q, u * pairs : (u + 2) * pairs, block:] = low
        for q in range(4):
            high, low = lhs[q, :, :block], lhs[q, :, block:]
            modes = jnp.dot(high, joint[0, q], preferred_element_type=F32)
            modes = modes + jnp.dot(low, joint[0, q], preferred_element_type=F32)
            modes = modes + jnp.dot(high, joint[1, q], preferred_element_type=F32)
            spectrum[:, :, q * block : (q + 1) * block] = modes.reshape(points, pairs, block)

        @pl.when(step < n_pair - 1)
        def _():
            later = order(step + 1)
            move(mine, later, 0, me ^ (later * meets)).wait_recv()
            for m in range(1, meets):
                move(held.at[later, 0], later, m, me ^ m).start()

        acc = jnp.zeros((pairs, 128), F32)
        for t in range(plane // 128):
            even, odd, result = convolve(base, t)
            acc = add_energy(acc, even, odd, result)
            for q in range(centre):
                field[step, centre + q, :, t * 128 : (t + 1) * 128] = result[q] + result[centre + q]
                field[step, centre - 1 - q, :, t * 128 : (t + 1) * 128] = result[q] - result[centre + q]
        energy[...] = acc

        @pl.when(step == extra_step)
        def _():
            acc = energy[...]
            for t in range(plane // 128):
                acc = add_energy(acc, *convolve(extra_block * planes, t))
            energy[...] = acc

        occ_b = jnp.zeros((pairs, 128), F32)
        occ_a = jnp.zeros((pairs, 128), F32)
        for m in range(meets):
            partner = me ^ (chunk * meets + m)
            for b in range(per_owner):
                weight = occ_ref[partner * per_owner + b]
                occ_b = jnp.where(lax.rem(sub, per_a) == m * per_owner + b, weight, occ_b)
        for a in range(per_owner):
            occ_a = jnp.where(sub // per_a == a, occ_ref[me * per_owner + a], occ_a)

        @pl.when(step < n_pair - 1)
        def _():
            share = energy[...] * occ_a * occ_b
            for m in range(meets):
                row = jnp.sum(jnp.where(member == m, share, 0.0), axis=0, keepdims=True)
                tile[...] += jnp.where(slot_row == chunk * meets + m, row, 0.0)

        scale = jnp.concatenate([occ_b] * (plane // 128), axis=1)[None]
        partner_part[step] = right[pl.ds(base, planes)] * scale
        return carry

    lax.fori_loop(0, n_pair, step_body, 0)

    across = (((1,), (1,)), ((), ()))
    back = n_pair * planes * pairs
    for q in range(4):
        cut = slice(q * block, (q + 1) * block)
        high, low = pieces(field[:, :, :, cut].reshape(back, block), 2)
        value = lax.dot_general(high, joint[0, q], across, preferred_element_type=F32)
        value = value + lax.dot_general(low, joint[0, q], across, preferred_element_type=F32)
        value = value + lax.dot_general(high, joint[1, q], across, preferred_element_type=F32)
        spectrum[:, :, cut] = value.reshape(points, pairs, block)

    acc = tile[...]
    for x in range(1, n_pair):
        pair_copy(x).wait()
        acc = acc + pair_in[x]
    sums[...] = acc

    for j in range(planes):
        acc = [0.0] * 4
        for step in range(n_pair):
            part = [spectrum[step * planes + j, :, q * block : (q + 1) * block] for q in range(4)]
            s0, d0 = part[0] + part[1], part[0] - part[1]
            s1, d1 = part[2] + part[3], part[2] - part[3]
            for q, value in enumerate((s0 + s1, d0 + d1, s0 - s1, d0 - d1)):
                acc[q] = acc[q] + value * partner_part[step, j, :, q * block : (q + 1) * block]
        for q in range(4):
            total[j, :, q * block : (q + 1) * block] = acc[q]

    for x in range(1, n_band):
        band_copy(x).start()

    stack = []
    for a in range(per_owner):
        value = total[:, a * per_a, :]
        for o in range(1, per_a):
            value = value + total[:, a * per_a + o, :]
        stack.append(value)
    stacked = jnp.concatenate(pieces(jnp.concatenate(stack, axis=0), 3), axis=0)
    for v in range(2):
        cut = slice(v * 2 * block, (v + 1) * 2 * block)
        parts = lax.dot_general(stacked[:, cut], maps[v], across, preferred_element_type=F32)
        height = per_owner * planes
        result = parts[:height] + parts[height : 2 * height] + parts[2 * height :]
        out_ref[:, :, cut] = -result.reshape(per_owner, planes, 2 * block)

    acc = sums[...]
    for x in range(1, n_band):
        band_copy(x).wait()
        acc = acc + band_in[x]
    for s in range(meets):
        wanted = plan_ref[group * meets + s]
        value = jnp.sum(jnp.where(slot_row == wanted, acc, 0.0))
        slot_ref[s] = -value * (1.0 / (2.0 * n_band * per_owner * points**3))

    for m in range(1, meets):
        move(mine, 0, m, me ^ m).wait_send()

    def drain(step, carry):
        chunk = order(step)
        move(mine, chunk, 0, me ^ (chunk * meets)).wait_send()
        for m in range(1, meets):
            move(held.at[chunk, 0], chunk, m, me ^ m).wait_send()
        return carry

    lax.fori_loop(1, n_pair, drain, 0)


def solution(mesh):
    n_band, n_pair = mesh.shape["band"], mesh.shape["pair"]
    meets = n_band // n_pair

    def on_device(orbitals, ker, occupations, plan):
        per_owner, points, plane = orbitals.shape
        planes = points // n_pair
        pairs = per_owner * per_owner * meets
        block = plane // 4
        maps, joint, cosine = tables(points, planes)
        vmem = pl.BlockSpec(memory_space=pltpu.VMEM)
        smem = pl.BlockSpec(memory_space=pltpu.SMEM)
        hbm = pl.BlockSpec(memory_space=pltpu.HBM)
        dma = pltpu.SemaphoreType.DMA
        return pl.pallas_call(
            functools.partial(kernel, (n_band, n_pair, points, per_owner)),
            out_shape=(
                jax.ShapeDtypeStruct((per_owner, planes, plane), F32),
                jax.ShapeDtypeStruct((meets,), F32),
            ),
            in_specs=[hbm] * 7,
            out_specs=(vmem, smem),
            scratch_shapes=[
                pltpu.SMEM(plan.shape, jnp.int32),
                pltpu.SMEM(occupations.shape, F32),
                pltpu.VMEM(ker.shape, F32),
                pltpu.VMEM(cosine.shape, F32),
                pltpu.VMEM(orbitals.shape, BF16),
                pltpu.VMEM((n_pair, meets, per_owner, points, plane), BF16),
                pltpu.VMEM(maps.shape, BF16),
                pltpu.VMEM(joint.shape, BF16),
                pltpu.VMEM((points, pairs, plane), F32),
                pltpu.VMEM((points, pairs, plane), F32),
                pltpu.VMEM((cosine.shape[0], plane), F32),
                pltpu.VMEM((4, points * pairs, 2 * block), BF16),
                pltpu.VMEM((points, pairs, plane), F32),
                pltpu.VMEM((n_pair, planes, pairs, plane), F32),
                pltpu.VMEM((n_pair, planes, pairs, plane), F32),
                pltpu.VMEM((planes, pairs, plane), F32),
                pltpu.VMEM((pairs, 128), F32),
                pltpu.VMEM((n_band, 128), F32),
                pltpu.VMEM((n_band, 128), F32),
                pltpu.VMEM((n_band, n_band, 128), F32),
                pltpu.VMEM((n_pair, n_band, 128), F32),
                dma((7,)),
                dma((n_pair, meets)),
                dma((n_pair, meets)),
                dma((n_band,)),
                dma((n_band,)),
                dma((n_pair,)),
                dma((n_pair,)),
            ],
            compiler_params=pltpu.CompilerParams(
                collective_id=0, has_side_effects=True, vmem_limit_bytes=48 * 1024 * 1024
            ),
        )(*(
            pltpu.with_memory_space_constraint(value, pltpu.HBM)
            for value in (plan, occupations, orbitals, ker, jnp.asarray(cosine), jnp.asarray(maps), jnp.asarray(joint))
        ))

    return jax.shard_map(
        on_device,
        mesh=mesh,
        in_specs=(P("band", None, None), P(), P(), P()),
        out_specs=(P("band", "pair", None), P("pair")),
        check_vma=False,
    )
```
